32 devices in a mesh: frame: 4 (over x, core), tile: 8 (over z, y).
Axes of the slice: x: 2, y: 2, z: 4, core: 2. Of those that a mesh axis runs over, the one named last changes fastest.
Arguments:
- frames: bfloat16 [4, 64, 64, 2048], P('frame', None, 'tile'), may hold values from -6 to 6
- predict_w: bfloat16 [2, 4, 3, 3, 64, 64], replicated, may hold values from -0.25 to 0.25
- predict_b: float32 [2, 4, 64], replicated, may hold values from -2 to 2
- update_w: bfloat16 [2, 4, 3, 3, 64, 64], replicated, may hold values from -0.25 to 0.25
- update_b: float32 [2, 4, 64], replicated, may hold values from -2 to 2
Outputs:
- coefficients: bfloat16 [4, 64, 64, 2048], P('frame', None, 'tile')
The draws below stay inside these ranges and needn't reach their ends.
All inputs are finite; a program needn't handle non-finite values.
Results may differ from the reference program's by a relative error of at most 0.009.
Values may be sent and summed in bfloat16 or wider, within the bound.
A program may use at most 128 MiB of HBM per device.

```python
import jax
import jax.numpy as jnp
from jax import lax

C = 64
W = 2048
LAYERS = 4
FRAMES = 4
H = 64


def shard_levels(own_key, dims, shards, low, top_value):
    loudness, own = 1.0, jax.random.fold_in(own_key, 6)
    for dim, blocks in shards:
        heights = jnp.exp(jax.random.uniform(jax.random.fold_in(own, dim), (blocks,), jnp.float32, low / len(shards), top_value / len(shards)))
        loudness = loudness * jnp.repeat(heights, dims[dim] // blocks).reshape([-1 if axis == dim else 1 for axis in range(len(dims))])
    return loudness


def normal_values(stream_key, dims, width, reach, cuts=(), held_as=jnp.bfloat16):
    array = jax.random.normal(stream_key, dims, jnp.float32) * width
    if len(cuts) > 0:
        array = shard_levels(stream_key, dims, cuts, -0.22, 0.18) * array
    return jnp.clip(array, min=-reach, max=reach).astype(held_as)


def setup_inputs(seed: int = 0) -> dict:
    keys = jax.random.split(jax.random.key(seed), 6)
    return {
        "frames": normal_values(keys[0], (FRAMES, C, H, W), 1.0, 6.0, ((0, 4), (2, 8))),
        "predict_w": normal_values(keys[1], (2, LAYERS, 3, 3, C, C), (9 * C) ** -0.5, 0.25),
        "predict_b": normal_values(keys[2], (2, LAYERS, C), 0.3, 2.0, (), jnp.float32),
        "update_w": normal_values(keys[3], (2, LAYERS, 3, 3, C, C), (9 * C) ** -0.5, 0.25),
        "update_b": normal_values(keys[4], (2, LAYERS, C), 0.3, 2.0, (), jnp.float32),
    }


def conv_layer(field, kernel, bias_row):
    weights = jnp.transpose(kernel.astype(jnp.float32), (2, 3, 0, 1))
    result = lax.conv_general_dilated(field, weights, (1, 1), ((1, 1), (1, 1)), dimension_numbers=("NCHW", "OIHW", "NCHW"), precision=lax.Precision.HIGHEST)
    return result + bias_row[None, :, None, None]


def network(field, kernels, biases):
    hidden = field.astype(jnp.float32)
    for layer_index in range(LAYERS):
        result = conv_layer(hidden, kernels[layer_index], biases[layer_index])
        if layer_index < LAYERS - 1:
            rounded = lax.optimization_barrier(jnp.maximum(result, 0.0).astype(jnp.bfloat16))
            hidden = rounded.astype(jnp.float32)
    return result


def reference(frames, predict_w, predict_b, update_w, update_b):
    even_frames = frames[0::2]
    odd_frames = frames[1::2]
    high_one = (odd_frames.astype(jnp.float32) - network(even_frames, predict_w[0], predict_b[0])).astype(jnp.bfloat16)
    low_one = (even_frames.astype(jnp.float32) + network(high_one, update_w[0], update_b[0])).astype(jnp.bfloat16)
    low_even = low_one[0::2]
    low_odd = low_one[1::2]
    high_two = (low_odd.astype(jnp.float32) - network(low_even, predict_w[1], predict_b[1])).astype(jnp.bfloat16)
    low_two = (low_even.astype(jnp.float32) + network(high_two, update_w[1], update_b[1])).astype(jnp.bfloat16)
    stacked = jnp.stack([low_two, high_one[0::2], high_two, high_one[1::2]], axis=1)
    return stacked.reshape(frames.shape)
```

```python
import functools

import jax
import jax.numpy as jnp
from jax import lax
from jax.experimental import pallas as pl
from jax.experimental.pallas import tpu as pltpu
from jax.sharding import PartitionSpec as P

LANES = 128


def network_kernel(total_rows, sign, row_ref, x_ref, base_ref, w_ref, b_ref, out_ref, a_ref, c_ref):
    layers = w_ref.shape[0]
    rows, channels, width = x_ref.shape
    first_row = row_ref[0]
    column = lax.broadcasted_iota(jnp.int32, (2 * channels, width), 1)
    source = x_ref
    for layer in range(layers):
        rows -= 2
        last = layer == layers - 1
        target = out_ref if last else (a_ref, c_ref)[layer % 2]

        def pair(i, carry, source=source, target=target, layer=layer, last=last):
            x = source[pl.ds(2 * i, 4)].reshape(4 * channels, width)
            acc = jnp.dot(w_ref[layer], x, preferred_element_type=jnp.float32)
            group = 2 * channels
            left = pltpu.roll(acc[:group], 1, 1)
            right = pltpu.roll(acc[2 * group :], width - 1, 1)
            y = (
                acc[group : 2 * group]
                + jnp.where(column == 0, 0.0, left)
                + jnp.where(column == width - 1, 0.0, right)
                + b_ref[layer]
            )
            for p in range(2):
                part = y[p * channels : (p + 1) * channels]
                if last:
                    base = base_ref[2 * i + p].astype(jnp.float32)
                    part = base + part if sign > 0 else base - part
                else:
                    g = first_row + layer + 1 + 2 * i + p
                    inside = jnp.logical_and(g >= 0, g < total_rows)
                    part = jnp.where(inside, jnp.maximum(part, 0.0), 0.0)
                target[2 * i + p] = part.astype(jnp.bfloat16)
            return carry

        lax.fori_loop(0, rows // 2, pair, 0)
        source = target


def network(x, base, first_row, total_rows, weights, bias, sign):
    rows, channels, width = x.shape
    layers = weights.shape[0]
    macs = sum(rows - 2 * (k + 1) for k in range(layers)) * width * channels * channels * 12
    vmem = pl.BlockSpec(memory_space=pltpu.VMEM)
    return pl.pallas_call(
        functools.partial(network_kernel, total_rows, sign),
        out_shape=jax.ShapeDtypeStruct(base.shape, jnp.bfloat16),
        in_specs=[pl.BlockSpec(memory_space=pltpu.SMEM), vmem, vmem, vmem, vmem],
        out_specs=vmem,
        scratch_shapes=[
            pltpu.VMEM((rows - 2, channels, width), jnp.bfloat16),
            pltpu.VMEM((rows - 4, channels, width), jnp.bfloat16),
        ],
        compiler_params=pltpu.CompilerParams(vmem_limit_bytes=40 * 1024 * 1024),
        cost_estimate=pl.CostEstimate(
            flops=2 * macs, bytes_accessed=2 * (x.size + 2 * base.size), transcendentals=0
        ),
    )(first_row, x, base, weights, bias)


def pair_weights(kernels):
    lead = kernels.ndim - 4
    placed = []
    for p in range(2):
        pads = [(0, 0)] * kernels.ndim
        pads[lead] = (p, 1 - p)
        placed.append(jnp.pad(kernels, pads))
    stacked = jnp.stack(placed, axis=lead)
    order = tuple(range(lead)) + tuple(lead + k for k in (2, 0, 3, 1, 4))
    moved = jnp.transpose(stacked, order)
    shape = moved.shape
    return moved.reshape(
        shape[:lead] + (shape[lead] * shape[lead + 1] * shape[lead + 2], shape[lead + 3] * shape[lead + 4])
    )


def local(frames, predict_w, predict_b, update_w, update_b):
    layers = predict_w.shape[1]
    own = jnp.transpose(frames[0], (1, 0, 2))
    own_rows, channels, width = own.shape
    half = own_rows // 2
    frame_count = lax.axis_size("frame")
    tile_count = lax.axis_size("tile")
    total_rows = own_rows * tile_count
    position = lax.axis_index("frame")
    tile = lax.axis_index("tile")
    core = position % 2
    is_odd = core == 1
    upper = position // 2 % 2
    is_upper = upper == 1
    devices = [(f, t) for f in range(frame_count) for t in range(tile_count)]

    def send(x, target):
        pairs = []
        for f, t in devices:
            to = target(f, t)
            if to is not None and 0 <= to[1] < tile_count:
                pairs.append((f * tile_count + t, to[0] * tile_count + to[1]))
        return lax.ppermute(x, ("frame", "tile"), pairs)

    def swap_core(x):
        return send(x, lambda f, t: (f ^ 1, t))

    def swap_halo(x):
        return send(x, lambda f, t: (f ^ 1, t + 1 if f % 2 else t - 1))

    predict_m, update_m = pair_weights(predict_w), pair_weights(update_w)

    def wide_bias(b):
        return jnp.concatenate([b, b], axis=-1)[..., None]

    predict_v, update_v = wide_bias(predict_b), wide_bias(update_b)
    first_row = (tile * own_rows + core * half - layers).astype(jnp.int32)[None]

    def around(x, other, halo):
        return jnp.concatenate(
            [jnp.where(is_odd, other, halo), x, jnp.where(is_odd, halo, other)], axis=0
        )

    top, bottom = own[:half], own[half:]
    down = send(bottom, lambda f, t: (f, t + 1) if f % 2 == 0 else None)
    up = send(top, lambda f, t: (f + 1, t - 1) if f % 2 == 0 else None)
    got_top = swap_core(top)
    got_bottom = send(bottom, lambda f, t: (f + 1, t) if f % 2 == 0 else None)
    even_field = jnp.concatenate(
        [
            jnp.where(is_odd, got_top, down),
            jnp.where(is_odd, got_bottom, top),
            jnp.where(is_odd, up, bottom),
        ],
        axis=0,
    )
    odd_half = jnp.where(is_odd, bottom, got_top)
    even_half = even_field[layers : layers + half]
    high = network(even_field, odd_half, first_row, total_rows, predict_m[0], predict_v[0], -1)
    high_halo = swap_halo(high)
    high_other = swap_core(high)
    low = network(
        around(high, high_other, high_halo), even_half, first_row, total_rows,
        update_m[0], update_v[0], 1,
    )

    part = width // 2
    block = part + LANES
    give = jnp.where(is_upper, low[:, :, :block], low[:, :, width - block :])
    keep = jnp.where(is_upper, low[:, :, width - block :], low[:, :, :block])
    got = send(give, lambda f, t: (f ^ 2, t))
    low_even = jnp.where(is_upper, got, keep)
    low_odd = jnp.where(is_upper, keep, got)
    even_halo = swap_halo(low_even)
    even_other = swap_core(low_even)
    high_two = network(
        around(low_even, even_other, even_halo), low_odd, first_row, total_rows,
        predict_m[1], predict_v[1], -1,
    )
    two_halo = swap_halo(high_two)
    two_other = swap_core(high_two)

    def trimmed(x):
        return jnp.where(is_upper, x[:, :, block - part :], x[:, :, :part])

    high_mine, high_theirs = trimmed(high_two), trimmed(two_other)
    high_block = jnp.concatenate([high_mine, high_theirs], axis=0)
    high_left = send(high_block, lambda f, t: (f + 2, t) if f % 4 == 0 else None)
    low_two = network(
        around(high_two, two_other, two_halo), low_even, first_row, total_rows,
        update_m[1], update_v[1], 1,
    )
    low_mine = trimmed(low_two)
    low_theirs = send(low_mine, lambda f, t: (f - 1, t) if f % 4 == 1 else None)
    right_top = send(low_mine, lambda f, t: (f - 2, t) if f % 4 == 2 else None)
    right_bottom = send(low_mine, lambda f, t: (f - 3, t) if f % 4 == 3 else None)
    low_left = jnp.concatenate([low_mine, low_theirs], axis=0)
    low_right = jnp.concatenate([right_top, right_bottom], axis=0)
    second = jnp.concatenate(
        [jnp.where(is_upper, high_left, low_left), jnp.where(is_upper, high_block, low_right)], axis=2
    )
    first = jnp.concatenate([high_other, high], axis=0)
    chosen = jnp.where(is_odd, first, second)
    return jnp.transpose(chosen, (1, 0, 2))[None]


def solution(mesh):
    in_specs = (P("frame", None, "tile", None), P(), P(), P(), P())
    out_specs = P("frame", None, "tile", None)
    return jax.shard_map(local, mesh=mesh, in_specs=in_specs, out_specs=out_specs, check_vma=False)
```

```python
import functools

import jax
import jax.numpy as jnp
from jax import lax
from jax.experimental import pallas as pl
from jax.experimental.pallas import tpu as pltpu
from jax.sharding import PartitionSpec as P

LANES = 128
MESSAGES = (
    "down0", "down1", "up0", "up1", "even0", "even1", "odd",
    "hs0", "hs1", "hh0", "hh1", "x", "fs", "fh", "gs", "gh", "hl", "l1", "l2", "l3",
)
SLOT = {name: k for k, name in enumerate(MESSAGES)}
LOCAL = ("own", "base", "keep", "out", "out2")
LSLOT = {name: k for k, name in enumerate(LOCAL)}


def build_weights(k_ref, level, w_ref):
    layers, channels = k_ref.shape[1], k_ref.shape[5]
    w_ref[...] = jnp.zeros_like(w_ref)
    for layer in range(layers):
        for s in range(3):
            for p in range(2):
                top = (2 * s + p) * channels
                for r in range(3):
                    q = r + p
                    w_ref[layer, top : top + channels, q * channels : (q + 1) * channels] = k_ref[
                        level, layer, r, s
                    ]


def kernel(tiles, own, pw, uw, pb, ub, out, e, h, b1, low, f2, h2, o2, l2, wa, wb, wc, wd, a_ref, c_ref, send_sem, recv_sem, local_sem):
    own_rows, channels, width = own.shape
    half = own_rows // 2
    layers = pw.shape[1]
    part = width // 2
    block = part + LANES
    f = lax.axis_index("frame")
    t = lax.axis_index("tile")
    core = lax.rem(f, 2)
    upper = lax.rem(lax.div(f, 2), 2)
    partner = f + 1 - 2 * core
    across = f + 2 - 4 * upper
    diagonal = across + 1 - 2 * core
    has_up, has_down = t > 0, t < tiles - 1
    is_even, is_odd = core == 0, core == 1
    is_lower, is_upper = upper == 0, upper == 1
    first_row = t * own_rows + core * half - layers
    halo_tile = t + 2 * core - 1
    has_halo = jnp.logical_and(halo_tile >= 0, halo_tile < tiles)

    barrier = pltpu.get_barrier_semaphore()

    def greet(frame, tile):
        pl.semaphore_signal(
            barrier, inc=1, device_id={"frame": frame, "tile": tile},
            device_id_type=pl.DeviceIdType.MESH,
        )

    for frame in (partner, across, diagonal):
        greet(frame, t)
    for ok, tile in ((has_up, t - 1), (has_down, t + 1)):

        @pl.when(ok)
        def _(tile=tile):
            greet(f, tile)
            greet(partner, tile)

    def remote(name, src, dst, frame, tile):
        return pltpu.make_async_remote_copy(
            src_ref=src, dst_ref=dst, send_sem=send_sem.at[SLOT[name]], recv_sem=recv_sem.at[SLOT[name]],
            device_id={"frame": frame, "tile": tile}, device_id_type=pl.DeviceIdType.MESH,
        )

    def here(name, src, dst):
        return pltpu.make_async_copy(src, dst, local_sem.at[LSLOT[name]])

    @pl.when(jnp.logical_not(has_halo))
    def _():
        for ref in (e, h, f2, h2):
            ref[pl.ds(2 * half * core, half)] = jnp.zeros(
                (half,) + ref.shape[1:], ref.dtype
            )

    pl.semaphore_wait(barrier, 3 + 2 * has_up.astype(jnp.int32) + 2 * has_down.astype(jnp.int32))

    cut = (slice(0, block + LANES), slice(block + LANES, width))
    mine = slice(half, 2 * half)

    def downs(k):
        return remote(f"down{k}", own.at[half:, :, cut[k]], e.at[:half, :, cut[k]], f, t + 1)

    def ups(k):
        return remote(f"up{k}", own.at[:half, :, cut[k]], e.at[2 * half :, :, cut[k]], partner, t - 1)

    def evens(k):
        return remote(f"even{k}", own.at[:, :, cut[k]], e.at[: 2 * half, :, cut[k]], partner, t)

    odd = remote("odd", own.at[:half], b1, partner, t)
    own_copy = here("own", own, e.at[half:])
    base_copy = here("base", own.at[half:], b1)

    @pl.when(is_even)
    def _():
        for k in range(2):
            @pl.when(has_down)
            def _():
                downs(k).start()

            @pl.when(has_up)
            def _():
                ups(k).start()

            evens(k).start()
        own_copy.start()

    @pl.when(is_odd)
    def _():
        odd.start()
        base_copy.start()

    build_weights(pw, 0, wa)
    build_weights(uw, 0, wb)
    build_weights(pw, 1, wc)
    build_weights(uw, 1, wd)

    def network(src, base, dst, cols, keep, w_ref, b_ref, level, sign):
        size = cols.stop - cols.start
        column = lax.broadcasted_iota(jnp.int32, (1, size), 1)
        first, final = column == 0, column == size - 1
        rows = src.shape[0]
        source = src
        for layer in range(layers):
            rows -= 2
            last = layer == layers - 1
            target = dst if last else (a_ref, c_ref)[layer % 2]

            def pair(i, carry, source=source, target=target, layer=layer, last=last):
                span = cols if layer == 0 else slice(0, size)
                x = source[pl.ds(2 * i, 4), :, span].reshape(4 * channels, size)
                acc = jnp.dot(w_ref[layer], x, preferred_element_type=jnp.float32)
                group = 2 * channels
                left = pltpu.roll(acc[:group], 1, 1)
                right = pltpu.roll(acc[2 * group :], size - 1, 1)
                y = (
                    acc[group : 2 * group]
                    + jnp.where(first, 0.0, left)
                    + jnp.where(final, 0.0, right)
                    + b_ref[level, layer]
                )
                for p in range(2):
                    value = y[p * channels : (p + 1) * channels]
                    if last:
                        value = value[:, keep.start - cols.start : keep.stop - cols.start]
                        old = base[2 * i + p, :, keep].astype(jnp.float32)
                        value = old + value if sign > 0 else old - value
                        target[2 * i + p, :, keep] = value.astype(jnp.bfloat16)
                    else:
                        g = first_row + layer + 1 + 2 * i + p
                        inside = jnp.logical_and(g >= 0, g < tiles * own_rows)
                        value = jnp.where(inside, jnp.maximum(value, 0.0), 0.0)
                        target[2 * i + p, :, 0:size] = value.astype(jnp.bfloat16)
                return carry

            lax.fori_loop(0, rows // 2, pair, 0)
            source = target

    def swap(name, field, cols):
        piece = field.at[mine, :, cols]
        return remote(name, piece, field.at[pl.ds(2 * half * core, half), :, cols], partner, t)

    def swap_in(name, field, cols):
        piece = field.at[mine, :, cols]
        return remote(name, piece, field.at[pl.ds(2 * half * (1 - core), half), :, cols], partner, t)

    def halo(name, field, cols):
        piece = field.at[mine, :, cols]
        return remote(name, piece, field.at[pl.ds(2 * half * (1 - core), half), :, cols], partner, halo_tile)

    def halo_in(name, field, cols):
        piece = field.at[mine, :, cols]
        return remote(name, piece, field.at[pl.ds(2 * half * core, half), :, cols], partner, halo_tile)

    def share(kind, k, field, cols):
        @pl.when(has_halo)
        def _():
            halo(kind + "h" + k, field, cols).start()

        swap(kind + "s" + k, field, cols).start()

    def arrive(kind, k, field, cols):
        swap_in(kind + "s" + k, field, cols).wait_recv()

        @pl.when(has_halo)
        def _():
            halo_in(kind + "h" + k, field, cols).wait_recv()

    def sent(kind, k, field, cols):
        swap(kind + "s" + k, field, cols).wait_send()

        @pl.when(has_halo)
        def _():
            halo(kind + "h" + k, field, cols).wait_send()

    hcut = (slice(0, block), slice(block, width))
    for k in range(2):
        @pl.when(is_even)
        def _():
            if k == 0:
                own_copy.wait()
                odd.wait_recv()

            @pl.when(has_up)
            def _():
                downs(k).wait_recv()

        @pl.when(is_odd)
        def _():
            if k == 0:
                base_copy.wait()
            evens(k).wait_recv()

            @pl.when(has_down)
            def _():
                ups(k).wait_recv()

        reads = slice(0, block + LANES) if k == 0 else slice(part, width)
        network(e, b1, h.at[mine], reads, hcut[k], wa, pb, 0, -1)
        share("h", str(k), h, hcut[k])

    for k in range(2):
        arrive("h", str(k), h, hcut[k])
        reads = slice(0, block) if k == 0 else slice(width - block, width)
        keep = slice(0, part) if k == 0 else slice(part, width)
        network(h, e.at[mine], low, reads, keep, wb, ub, 0, 1)

    high_out = here("out", h.at[: 2 * half], out)
    left, right = slice(0, block), slice(width - block, width)
    give_even = remote("x", low.at[:, :, right], f2.at[mine], across, t)
    give_odd = remote("x", low.at[:, :, left], o2, across, t)
    keep_even = here("keep", low.at[:, :, left], f2.at[mine])
    keep_odd = here("keep", low.at[:, :, right], o2)
    every = slice(0, block)

    @pl.when(is_lower)
    def _():
        give_even.start()
        keep_even.start()
        keep_even.wait()

    @pl.when(is_upper)
    def _():
        give_odd.start()
        keep_odd.start()
        give_even.wait_recv()

    share("f", "", f2, every)

    @pl.when(is_odd)
    def _():
        high_out.start()

    arrive("f", "", f2, every)

    @pl.when(is_lower)
    def _():
        give_odd.wait_recv()

    @pl.when(is_upper)
    def _():
        keep_odd.wait()

    network(f2, o2, h2.at[mine], every, every, wc, pb, 1, -1)
    share("g", "", h2, every)
    arrive("g", "", h2, every)

    near, far = slice(0, part), slice(part, width)
    tail = slice(block - part, block)
    high_send = remote("hl", h2.at[half:, :, near], out.at[:, :, near], across, t)
    high_keep = here("out", h2.at[half:, :, tail], out.at[:, :, far])
    at_low = jnp.logical_and(is_even, is_lower)
    at_high = jnp.logical_and(is_even, is_upper)

    @pl.when(at_low)
    def _():
        high_send.start()

    @pl.when(at_high)
    def _():
        high_keep.start()

    network(h2, f2.at[mine], l2, every, every, wd, ub, 1, 1)

    low_keep = here("out2", l2.at[:, :, near], out.at[:half, :, near])
    first = remote("l1", l2.at[:, :, near], out.at[half:, :, near], partner, t)
    second = remote("l2", l2.at[:, :, tail], out.at[:half, :, far], across, t)
    third = remote("l3", l2.at[:, :, tail], out.at[half:, :, far], diagonal, t)

    @pl.when(at_low)
    def _():
        low_keep.start()
        first.wait_recv()
        second.wait_recv()
        third.wait_recv()
        low_keep.wait()
        high_send.wait_send()

    @pl.when(at_high)
    def _():
        second.start()
        high_keep.wait()
        high_send.wait_recv()
        second.wait_send()

    @pl.when(jnp.logical_and(is_odd, is_lower))
    def _():
        first.start()
        first.wait_send()

    @pl.when(jnp.logical_and(is_odd, is_upper))
    def _():
        third.start()
        third.wait_send()

    @pl.when(is_odd)
    def _():
        high_out.wait()
        odd.wait_send()

    @pl.when(is_even)
    def _():
        for k in range(2):
            @pl.when(has_down)
            def _():
                downs(k).wait_send()

            @pl.when(has_up)
            def _():
                ups(k).wait_send()

            evens(k).wait_send()

    @pl.when(is_lower)
    def _():
        give_even.wait_send()

    @pl.when(is_upper)
    def _():
        give_odd.wait_send()

    for k in range(2):
        sent("h", str(k), h, hcut[k])
    sent("f", "", f2, every)
    sent("g", "", h2, every)


def local(frames, predict_w, predict_b, update_w, update_b):
    own = jnp.transpose(frames[0], (1, 0, 2))
    own_rows, channels, width = own.shape
    half = own_rows // 2
    layers = predict_w.shape[1]
    block = width // 2 + LANES
    tiles = lax.axis_size("tile")

    def wide_bias(b):
        return jnp.concatenate([b, b], axis=-1)[..., None]

    vmem = pl.BlockSpec(memory_space=pltpu.VMEM)
    hbm = pl.BlockSpec(memory_space=pl.ANY)

    def buffer(rows, columns):
        return pltpu.VMEM((rows, channels, columns), jnp.bfloat16)

    weight = pltpu.VMEM((layers, 6 * channels, 4 * channels), jnp.bfloat16)
    result = pl.pallas_call(
        functools.partial(kernel, tiles),
        out_shape=jax.ShapeDtypeStruct(own.shape, jnp.bfloat16),
        in_specs=[hbm, vmem, vmem, vmem, vmem],
        out_specs=hbm,
        scratch_shapes=[
            buffer(3 * half, width), buffer(3 * half, width), buffer(half, width), buffer(half, width),
            buffer(3 * half, block), buffer(3 * half, block), buffer(half, block), buffer(half, block),
            weight, weight, weight, weight,
            buffer(3 * half - 2, block + LANES), buffer(3 * half - 4, block + LANES),
            pltpu.SemaphoreType.DMA((len(MESSAGES),)),
            pltpu.SemaphoreType.DMA((len(MESSAGES),)),
            pltpu.SemaphoreType.DMA((len(LOCAL),)),
        ],
        compiler_params=pltpu.CompilerParams(
            collective_id=0, has_side_effects=True, vmem_limit_bytes=60 * 1024 * 1024
        ),
    )(own, predict_w, update_w, wide_bias(predict_b), wide_bias(update_b))
    return jnp.transpose(result, (1, 0, 2))[None]


def solution(mesh):
    in_specs = (P("frame", None, "tile", None), P(), P(), P(), P())
    out_specs = P("frame", None, "tile", None)
    return jax.shard_map(local, mesh=mesh, in_specs=in_specs, out_specs=out_specs, check_vma=False)
```

```python
import functools

import jax
import jax.numpy as jnp
from jax import lax
from jax.experimental import pallas as pl
from jax.experimental.pallas import tpu as pltpu
from jax.sharding import PartitionSpec as P

LANES = 128
MESSAGES = (
    "down0", "down1", "up0", "up1", "even0", "even1", "odd",
    "hs0", "hs1", "hh0", "hh1", "x", "x2", "x3", "fs", "fh", "gs", "gh", "hl", "l1", "l2", "l3",
)
SLOT = {name: k for k, name in enumerate(MESSAGES)}
LOCAL = ("own", "base", "keep", "out", "out2")
LSLOT = {name: k for k, name in enumerate(LOCAL)}


def build_weights(k_ref, level, w_ref):
    layers, channels = k_ref.shape[1], k_ref.shape[5]
    w_ref[...] = jnp.zeros_like(w_ref)
    for layer in range(layers):
        for s in range(3):
            for p in range(2):
                top = (2 * s + p) * channels
                for r in range(3):
                    q = r + p
                    w_ref[layer, top : top + channels, q * channels : (q + 1) * channels] = k_ref[
                        level, layer, r, s
                    ]


def kernel(tiles, own, pw, uw, pb, ub, out, e, h, b1, low, f2, h2, o2, l2, wa, wb, wc, wd, a_ref, c_ref, d_ref, send_sem, recv_sem, local_sem):
    own_rows, channels, width = own.shape
    half = own_rows // 2
    layers = pw.shape[1]
    part = width // 2
    block = part + LANES
    f = lax.axis_index("frame")
    t = lax.axis_index("tile")
    core = lax.rem(f, 2)
    upper = lax.rem(lax.div(f, 2), 2)
    partner = f + 1 - 2 * core
    across = f + 2 - 4 * upper
    diagonal = across + 1 - 2 * core
    has_up, has_down = t > 0, t < tiles - 1
    is_even, is_odd = core == 0, core == 1
    is_lower, is_upper = upper == 0, upper == 1
    first_row = t * own_rows + core * half - layers
    halo_tile = t + 2 * core - 1
    has_halo = jnp.logical_and(halo_tile >= 0, halo_tile < tiles)

    barrier = pltpu.get_barrier_semaphore()

    def greet(frame, tile):
        pl.semaphore_signal(
            barrier, inc=1, device_id={"frame": frame, "tile": tile},
            device_id_type=pl.DeviceIdType.MESH,
        )

    for frame in (partner, across, diagonal):
        greet(frame, t)
    for ok, tile in ((has_up, t - 1), (has_down, t + 1)):

        @pl.when(ok)
        def _(tile=tile):
            greet(f, tile)
            greet(partner, tile)

    def remote(name, src, dst, frame, tile):
        return pltpu.make_async_remote_copy(
            src_ref=src, dst_ref=dst, send_sem=send_sem.at[SLOT[name]], recv_sem=recv_sem.at[SLOT[name]],
            device_id={"frame": frame, "tile": tile}, device_id_type=pl.DeviceIdType.MESH,
        )

    def here(name, src, dst):
        return pltpu.make_async_copy(src, dst, local_sem.at[LSLOT[name]])

    @pl.when(jnp.logical_not(has_halo))
    def _():
        for ref in (e, h, f2, h2):
            ref[pl.ds(2 * half * core, half)] = jnp.zeros(
                (half,) + ref.shape[1:], ref.dtype
            )

    pl.semaphore_wait(barrier, 3 + 2 * has_up.astype(jnp.int32) + 2 * has_down.astype(jnp.int32))

    cut = (slice(0, block + LANES), slice(block + LANES, width))
    mine = slice(half, 2 * half)

    def downs(k):
        return remote(f"down{k}", own.at[half:, :, cut[k]], e.at[:half, :, cut[k]], f, t + 1)

    def ups(k):
        return remote(f"up{k}", own.at[:half, :, cut[k]], e.at[2 * half :, :, cut[k]], partner, t - 1)

    def evens(k):
        return remote(f"even{k}", own.at[:, :, cut[k]], e.at[: 2 * half, :, cut[k]], partner, t)

    odd = remote("odd", own.at[:half], b1, partner, t)
    own_copy = here("own", own, e.at[half:])
    base_copy = here("base", own.at[half:], b1)

    @pl.when(is_even)
    def _():
        for k in range(2):
            @pl.when(has_down)
            def _():
                downs(k).start()

            @pl.when(has_up)
            def _():
                ups(k).start()

            evens(k).start()
        own_copy.start()

    @pl.when(is_odd)
    def _():
        odd.start()
        base_copy.start()

    build_weights(pw, 0, wa)
    build_weights(uw, 0, wb)
    build_weights(pw, 1, wc)
    build_weights(uw, 1, wd)

    def network(src, base, dst, cols, keep, w_ref, b_ref, level, sign, await_halo):
        size = cols.stop - cols.start
        column = lax.broadcasted_iota(jnp.int32, (1, size), 1)
        first, final = column == 0, column == size - 1
        hidden = (a_ref, c_ref, d_ref)

        def phase_step(phase, carry):
            @pl.when(phase == 1)
            def _():
                await_halo()

            source = src
            for layer in range(layers):
                count = (src.shape[0] - 2 * (layer + 1)) // 2
                free = max(half - (layer + 1), 0)
                last = layer == layers - 1
                target = dst if last else hidden[layer]

                def pair(i, carry, source=source, target=target, layer=layer, last=last):
                    span = cols if layer == 0 else slice(0, size)
                    x = source[pl.ds(2 * i, 4), :, span].reshape(4 * channels, size)
                    acc = jnp.dot(w_ref[layer], x, preferred_element_type=jnp.float32)
                    group = 2 * channels
                    left = pltpu.roll(acc[:group], 1, 1)
                    right = pltpu.roll(acc[2 * group :], size - 1, 1)
                    y = (
                        acc[group : 2 * group]
                        + jnp.where(first, 0.0, left)
                        + jnp.where(final, 0.0, right)
                        + b_ref[level, layer]
                    )
                    for p in range(2):
                        value = y[p * channels : (p + 1) * channels]
                        if last:
                            value = value[:, keep.start - cols.start : keep.stop - cols.start]
                            old = base[2 * i + p, :, keep].astype(jnp.float32)
                            value = old + value if sign > 0 else old - value
                            target[2 * i + p, :, keep] = value.astype(jnp.bfloat16)
                        else:
                            g = first_row + layer + 1 + 2 * i + p
                            inside = jnp.logical_and(g >= 0, g < tiles * own_rows)
                            value = jnp.where(inside, jnp.maximum(value, 0.0), 0.0)
                            target[2 * i + p, :, 0:size] = value.astype(jnp.bfloat16)
                    return carry

                begin = (1 - phase) * (1 - core) * (count - free) + phase * core * free
                amount = (1 - phase) * free + phase * (count - free)
                lax.fori_loop(begin, begin + amount, pair, 0)
                source = target
            return carry

        lax.fori_loop(0, 2, phase_step, 0)

    def swap(name, field, cols):
        piece = field.at[mine, :, cols]
        return remote(name, piece, field.at[pl.ds(2 * half * core, half), :, cols], partner, t)

    def swap_in(name, field, cols):
        piece = field.at[mine, :, cols]
        return remote(name, piece, field.at[pl.ds(2 * half * (1 - core), half), :, cols], partner, t)

    def halo(name, field, cols):
        piece = field.at[mine, :, cols]
        return remote(name, piece, field.at[pl.ds(2 * half * (1 - core), half), :, cols], partner, halo_tile)

    def halo_in(name, field, cols):
        piece = field.at[mine, :, cols]
        return remote(name, piece, field.at[pl.ds(2 * half * core, half), :, cols], partner, halo_tile)

    def share(kind, k, field, cols):
        @pl.when(has_halo)
        def _():
            halo(kind + "h" + k, field, cols).start()

        swap(kind + "s" + k, field, cols).start()

    def arrive_halo(kind, k, field, cols):
        @pl.when(has_halo)
        def _():
            halo_in(kind + "h" + k, field, cols).wait_recv()

    def sent(kind, k, field, cols):
        swap(kind + "s" + k, field, cols).wait_send()

        @pl.when(has_halo)
        def _():
            halo(kind + "h" + k, field, cols).wait_send()

    hcut = (slice(0, block), slice(block, width))
    for k in range(2):
        @pl.when(is_even)
        def _():
            if k == 0:
                own_copy.wait()
                odd.wait_recv()

        @pl.when(is_odd)
        def _():
            if k == 0:
                base_copy.wait()
            evens(k).wait_recv()

        def frame_halo(k=k):
            @pl.when(jnp.logical_and(is_even, has_up))
            def _():
                downs(k).wait_recv()

            @pl.when(jnp.logical_and(is_odd, has_down))
            def _():
                ups(k).wait_recv()

        reads = slice(0, block + LANES) if k == 0 else slice(part, width)
        network(e, b1, h.at[mine], reads, hcut[k], wa, pb, 0, -1, frame_halo)
        share("h", str(k), h, hcut[k])

    left, right = slice(0, block), slice(width - block, width)
    near, far = slice(0, part), slice(part, width)
    rest = slice(part, block)
    tail = slice(block - part, block)
    give_near = remote("x", low.at[:, :, near], f2.at[mine, :, near], across, t)
    give_rest = remote("x2", low.at[:, :, rest], f2.at[mine, :, rest], across, t)
    give_odd = remote("x3", low.at[:, :, right], o2, across, t)
    keep_even = here("keep", low.at[:, :, right], f2.at[mine])
    keep_odd = here("keep", low.at[:, :, left], o2)
    for k in range(2):
        swap_in("hs" + str(k), h, hcut[k]).wait_recv()
        reads = slice(0, block) if k == 0 else slice(width - block, width)

        def high_halo(k=k):
            arrive_halo("h", str(k), h, hcut[k])

        network(h, e.at[mine], low, reads, (near, far)[k], wb, ub, 0, 1, high_halo)

        @pl.when(is_lower)
        def _():
            (give_near, give_rest)[k].start()

    high_out = here("out", h.at[: 2 * half], out)
    every = slice(0, block)

    @pl.when(is_lower)
    def _():
        keep_even.start()
        keep_even.wait()

    @pl.when(is_upper)
    def _():
        give_odd.start()
        keep_odd.start()
        give_near.wait_recv()
        give_rest.wait_recv()

    share("f", "", f2, every)

    @pl.when(is_odd)
    def _():
        high_out.start()

    @pl.when(is_lower)
    def _():
        give_odd.wait_recv()

    @pl.when(is_upper)
    def _():
        keep_odd.wait()

    swap_in("fs", f2, every).wait_recv()
    network(f2, o2, h2.at[mine], every, every, wc, pb, 1, -1, lambda: arrive_halo("f", "", f2, every))
    share("g", "", h2, every)
    swap_in("gs", h2, every).wait_recv()

    high_send = remote("hl", h2.at[half:, :, tail], out.at[:, :, far], across, t)
    high_keep = here("out", h2.at[half:, :, near], out.at[:, :, near])
    at_low = jnp.logical_and(is_even, is_lower)
    at_high = jnp.logical_and(is_even, is_upper)

    @pl.when(at_low)
    def _():
        high_send.start()

    @pl.when(at_high)
    def _():
        high_keep.start()

    network(h2, f2.at[mine], l2, every, every, wd, ub, 1, 1, lambda: arrive_halo("g", "", h2, every))

    low_keep = here("out2", l2.at[:, :, tail], out.at[:half, :, far])
    first = remote("l1", l2.at[:, :, tail], out.at[half:, :, far], partner, t)
    second = remote("l2", l2.at[:, :, near], out.at[:half, :, near], across, t)
    third = remote("l3", l2.at[:, :, near], out.at[half:, :, near], diagonal, t)

    @pl.when(at_low)
    def _():
        low_keep.start()
        first.wait_recv()
        second.wait_recv()
        third.wait_recv()
        low_keep.wait()
        high_send.wait_send()

    @pl.when(at_high)
    def _():
        second.start()
        high_keep.wait()
        high_send.wait_recv()
        second.wait_send()

    @pl.when(jnp.logical_and(is_odd, is_lower))
    def _():
        first.start()
        first.wait_send()

    @pl.when(jnp.logical_and(is_odd, is_upper))
    def _():
        third.start()
        third.wait_send()

    @pl.when(is_odd)
    def _():
        high_out.wait()
        odd.wait_send()

    @pl.when(is_even)
    def _():
        for k in range(2):
            @pl.when(has_down)
            def _():
                downs(k).wait_send()

            @pl.when(has_up)
            def _():
                ups(k).wait_send()

            evens(k).wait_send()

    @pl.when(is_lower)
    def _():
        give_near.wait_send()
        give_rest.wait_send()

    @pl.when(is_upper)
    def _():
        give_odd.wait_send()

    for k in range(2):
        sent("h", str(k), h, hcut[k])
    sent("f", "", f2, every)
    sent("g", "", h2, every)


def local(frames, predict_w, predict_b, update_w, update_b):
    own = jnp.transpose(frames[0], (1, 0, 2))
    own_rows, channels, width = own.shape
    half = own_rows // 2
    layers = predict_w.shape[1]
    block = width // 2 + LANES
    tiles = lax.axis_size("tile")

    def wide_bias(b):
        return jnp.concatenate([b, b], axis=-1)[..., None]

    vmem = pl.BlockSpec(memory_space=pltpu.VMEM)
    hbm = pl.BlockSpec(memory_space=pl.ANY)

    def buffer(rows, columns):
        return pltpu.VMEM((rows, channels, columns), jnp.bfloat16)

    weight = pltpu.VMEM((layers, 6 * channels, 4 * channels), jnp.bfloat16)
    result = pl.pallas_call(
        functools.partial(kernel, tiles),
        out_shape=jax.ShapeDtypeStruct(own.shape, jnp.bfloat16),
        in_specs=[hbm, vmem, vmem, vmem, vmem],
        out_specs=hbm,
        scratch_shapes=[
            buffer(3 * half, width), buffer(3 * half, width), buffer(half, width), buffer(half, width),
            buffer(3 * half, block), buffer(3 * half, block), buffer(half, block), buffer(half, block),
            weight, weight, weight, weight,
            buffer(3 * half - 2, block + LANES), buffer(3 * half - 4, block + LANES),
            buffer(3 * half - 6, block + LANES),
            pltpu.SemaphoreType.DMA((len(MESSAGES),)),
            pltpu.SemaphoreType.DMA((len(MESSAGES),)),
            pltpu.SemaphoreType.DMA((len(LOCAL),)),
        ],
        compiler_params=pltpu.CompilerParams(
            collective_id=0, has_side_effects=True, vmem_limit_bytes=60 * 1024 * 1024
        ),
    )(own, predict_w, update_w, wide_bias(predict_b), wide_bias(update_b))
    return jnp.transpose(result, (1, 0, 2))[None]


def solution(mesh):
    in_specs = (P("frame", None, "tile", None), P(), P(), P(), P())
    out_specs = P("frame", None, "tile", None)
    return jax.shard_map(local, mesh=mesh, in_specs=in_specs, out_specs=out_specs, check_vma=False)
```
